32 devices in a mesh: seq: 32 (over z, y, x, core), head: 1.
Axes of the slice: x: 2, y: 2, z: 4, core: 2. Of those that a mesh axis runs over, the one named last changes fastest.
Arguments:
- queries: bfloat16 [4096, 128], P('seq'), may hold values from -6 to 6
- key_rows: bfloat16 [4096, 128], P('seq'), may hold values from -0.01171875 to 0.01171875
- values: bfloat16 [4096, 5120], P('seq', 'head'), may hold values from -6 to 6
- gate_rows: bfloat16 [4096, 5120], P('seq', 'head'), may hold values from -6 to 6
- log_decay: float32 [4096, 80], P('seq', 'head'), may hold values from -0.69 to 0
- skip_gain: float32 [80], P('head'), may hold values from 0.3 to 4.2
- lam_index: int32 [4096], P('seq'), may hold values from 0 to 63
- segments: int32 [4096], P('seq'), may hold values from 0 to 127, never falling along the last dimension, each value on 1 to 64 neighbouring positions
- lam_table: float32 [64, 7, 80], P(None, None, 'head'), may hold values from 0.2 to 2
- norm_gain: float32 [5120], P('head'), may hold values from 0.25 to 1.75
- out_proj: bfloat16 [5120, 2560], P('head', 'seq'), may hold values from -0.078125 to 0.078125
Outputs:
- mixer_out: bfloat16 [4096, 2560], P(('seq', 'head'))
The draws below stay inside these ranges and needn't reach their ends.
Inputs may be any that keep to these rules, and one draw needn't show every extreme that they name: `segments`: stretch numbers never fall along the sequence; each stretch has 1 to 64 tokens.
All inputs are finite; a program needn't handle non-finite values.
Results may differ from the reference program's by a relative error of at most 0.012.
Values may be sent and summed in bfloat16 or wider, within the bound.
A program may use at most 128 MiB of HBM per device.

```python
import math
import jax
import jax.numpy as jnp
import numpy as np
from jax import lax

DM = 2560
HEAD_TOTAL = 80
HEAD_DIM = 64
STATE = 128
TOK_DEV = 128
CLASSES = 64
LOGS = 5
LEVELS = 7
DI = 5120
GROUP_COLS = 5120
TOKEN_TOTAL = 4096


def draw_log_decay(key, part):
    key_sequence = jax.random.split(jax.random.fold_in(key, 11), 7)
    fast_share = 0.35
    fast_heads = jax.random.bernoulli(key_sequence[0], fast_share, (HEAD_TOTAL,))
    fast_rate = jax.random.uniform(key_sequence[1], (HEAD_TOTAL,), jnp.float32, 1.0 / 50.0, 1.0 / 30.0)
    slow_total = jax.random.uniform(key_sequence[2], (HEAD_TOTAL,), jnp.float32, 0.05, 0.4)
    baseline_rate = jnp.where(fast_heads, fast_rate, slow_total / TOKEN_TOTAL)
    token_multiplier = jnp.exp(jax.random.uniform(key_sequence[3], (TOKEN_TOTAL, HEAD_TOTAL), jnp.float32, -math.log(2.0), math.log(2.0)))
    shard_multiplier = jnp.exp(jax.random.uniform(key_sequence[4], (TOKEN_TOTAL // TOK_DEV, HEAD_TOTAL), jnp.float32, -math.log(2.0), math.log(2.0)))
    shard_multiplier = jnp.repeat(shard_multiplier, TOK_DEV, axis=0)
    spike_positions = jax.random.randint(key_sequence[5], (2,), 0, TOKEN_TOTAL)
    spike_rows = jnp.any(jnp.arange(TOKEN_TOTAL, dtype=jnp.int32)[:, None] == spike_positions[None, :], axis=1)
    spike_loss = jnp.log(1.0 - jax.random.uniform(key_sequence[6], (TOKEN_TOTAL, HEAD_TOTAL), jnp.float32, 0.2, 0.45))
    final_result = -baseline_rate[None, :] * token_multiplier * shard_multiplier + jnp.where(spike_rows[:, None], spike_loss, 0.0)
    return jnp.maximum(final_result, -0.69).astype(jnp.float32)


def draw_skip_gain(key, part):
    base_gain = jnp.exp(jnp.linspace(math.log(0.5), math.log(2.5), HEAD_TOTAL))
    jitter = jax.random.uniform(jax.random.fold_in(key, 23), (HEAD_TOTAL,), jnp.float32, -0.3, 0.3)
    return (base_gain * jnp.exp(jitter)).astype(jnp.float32)


def with_ends(drawn, rng, least, top_value):
    index_at = [jax.random.randint(jax.random.fold_in(rng, axis), (), 0, length) for axis, length in enumerate(drawn.shape)]
    main_axis = drawn.shape.index(max(drawn.shape))
    beside = index_at[:main_axis] + [(index_at[main_axis] + 1) % drawn.shape[main_axis]] + index_at[main_axis + 1:]
    return drawn.at[tuple(index_at)].set(least).at[tuple(beside)].set(top_value)


def levels(rng, shape, pieces, least, top_value):
    level = 1.0
    for position, shards_of in pieces:
        steps = jax.random.uniform(jax.random.fold_in(jax.random.fold_in(rng, 6), position), (shards_of,), jnp.float32, least / len(pieces), top_value / len(pieces))
        level = level * jnp.repeat(jnp.exp(steps), shape[position] // shards_of).reshape((-1,) + (1,) * (len(shape) - 1 - position))
    return level


def length_profile(number_of, total, bound, lean):
    weights = [(1 << 20) // math.isqrt(standing ** lean) + 1 for standing in range(2, number_of + 1)]
    surplus, holding = total - bound - (number_of - 1), [1] * (number_of - 1)
    while surplus > 0:
        movable = [i for i in range(number_of - 1) if holding[i] < bound]
        whole, remaining = sum([weights[i] for i in movable]), surplus
        for i in movable:
            addition = min(bound - holding[i], max(1, remaining * weights[i] // whole), surplus)
            holding[i] = holding[i] + addition
            surplus = surplus - addition
    return np.array([bound] + holding)


def uneven(own_key, count, total, bound, lean):
    if count == 2:
        one = jax.random.randint(own_key, (), max(1, total - bound), min(bound, total - 1) + 1)
        return jnp.stack([one, total - one])
    sizes = jnp.asarray(length_profile(count, total, bound, lean), jnp.int32)
    twos = (count - 1) // 2
    giver, sink = sizes[1:1 + 2 * twos:2], sizes[2:2 + 2 * twos:2]
    room = jnp.minimum(giver - 1, bound - sink)
    passed = jax.random.randint(jax.random.fold_in(own_key, 1), (twos,), 0, 1 << 20) % (room + 1)
    sizes = sizes.at[1:1 + 2 * twos:2].set(giver - passed).at[2:2 + 2 * twos:2].set(sink + passed)
    return sizes[jax.random.permutation(jax.random.fold_in(own_key, 2), count)]


def centred(own_key, shape, deviation, reach, shards=(), kind=jnp.bfloat16):
    gain = levels(own_key, shape, shards, -0.22, 0.18) if shards else 1.0
    drawn = jax.random.normal(own_key, shape, jnp.float32) * deviation * gain
    return jnp.minimum(jnp.maximum(drawn, -reach), reach).astype(kind)


def setup_inputs(seed: int = 0) -> dict:
    key_list = jax.random.split(jax.random.key(seed), 12)
    return {
        "queries": centred(key_list[0], (TOKEN_TOTAL, STATE), 1.0, 6.0, ((0, 32),)),
        "key_rows": centred(key_list[1], (TOKEN_TOTAL, STATE), ((STATE * TOKEN_TOTAL // 2) ** -0.5), 0.01171875, ((0, 32),)),
        "values": centred(key_list[2], (TOKEN_TOTAL, DI), 1.0, 6.0, ((0, 32),)),
        "gate_rows": centred(key_list[3], (TOKEN_TOTAL, DI), 1.0, 6.0, ((0, 32),)),
        "log_decay": draw_log_decay(jax.random.fold_in(key_list[11], 71), 0),
        "skip_gain": draw_skip_gain(jax.random.fold_in(key_list[11], 71), 0),
        "lam_index": with_ends(jax.random.randint(key_list[6], (TOKEN_TOTAL,), 0, CLASSES), jax.random.fold_in(key_list[6], 1), 0, CLASSES - 1).astype(jnp.int32),
        "segments": jnp.searchsorted(jnp.cumsum(uneven(key_list[7], TOKEN_TOTAL // 32, TOKEN_TOTAL, 64, 1)), jnp.arange(TOKEN_TOTAL), side="right").astype(jnp.int32),
        "lam_table": jnp.clip(jnp.exp(jax.random.uniform(key_list[8], (CLASSES, LEVELS, HEAD_TOTAL), jnp.float32, math.log(0.2), math.log(2.0))), 0.2, 2.0),
        "norm_gain": jnp.clip(1.0 + 0.15 * jax.random.normal(key_list[9], (DI,), jnp.float32), 0.25, 1.75),
        "out_proj": centred(key_list[10], (DI, DM), DI ** -0.5, 0.078125, ((1, 32),)),
    }


epsilon = 1e-05
highest = lax.Precision.HIGHEST

def level_up(group_bf, bounds, level_pos, head_dim):
    pair_count = group_bf.shape[0] // 2
    width = 2 ** level_pos
    upper_start = (2 * jnp.arange(pair_count, dtype=jnp.int32) + 1) * width
    span = bounds[upper_start + width] - bounds[upper_start]
    pairs = group_bf.reshape(pair_count, 2, group_bf.shape[1], group_bf.shape[2]).astype(jnp.float32)
    factor = jnp.repeat(jnp.exp(span), head_dim, axis=1)[:, None, :]
    return (pairs[:, 1] + factor * pairs[:, 0]).astype(jnp.bfloat16)

def reference(queries, key_rows, values, gate_rows, log_decay, skip_gain, lam_index, segments, lam_table, norm_gain, out_proj):
    shard_count = TOKEN_TOTAL // TOK_DEV
    q_all = queries.reshape(shard_count, TOK_DEV, STATE)
    k_all = key_rows.reshape(shard_count, TOK_DEV, STATE)
    v_all = values.reshape(shard_count, TOK_DEV, DI)
    z_all = gate_rows.reshape(shard_count, TOK_DEV, DI)
    cum_all = jnp.cumsum(log_decay.reshape(shard_count, TOK_DEV, HEAD_TOTAL), axis=1)
    onehot = (lam_index[:, None] == jnp.arange(CLASSES, dtype=jnp.int32)[None, :]).astype(jnp.float32)
    level_wts = jnp.dot(onehot, lam_table.reshape(CLASSES, LEVELS * HEAD_TOTAL), precision=highest)
    level_wts = level_wts.reshape(shard_count, TOK_DEV, LEVELS, HEAD_TOTAL)
    seg_all = segments.reshape(shard_count, TOK_DEV)

    def end_state(args):
        k_blk, v_blk, c_blk = args
        decay_end = jnp.repeat(jnp.exp(c_blk[-1][None, :] - c_blk), HEAD_DIM, axis=1)
        decayed = (v_blk.astype(jnp.float32) * decay_end).astype(jnp.bfloat16)
        return jnp.dot(k_blk.T, decayed, preferred_element_type=jnp.float32).astype(jnp.bfloat16)
    end_states = lax.map(end_state, (k_all, v_all, cum_all))
    bounds = jnp.concatenate([jnp.zeros((1, HEAD_TOTAL), jnp.float32), jnp.cumsum(cum_all[:, -1, :], axis=0)], axis=0)
    group_levels = [end_states]
    for level_pos in range(LOGS - 1):
        group_levels.append(level_up(group_levels[-1], bounds, level_pos, HEAD_DIM))
    shard_ids = jnp.arange(shard_count, dtype=jnp.int32)
    positions = jnp.arange(TOK_DEV, dtype=jnp.int32)
    causal = positions[:, None] >= positions[None, :]

    def shard_out(args):
        shard_pos, q_blk, k_blk, v_blk, z_blk, c_blk, w_blk, s_blk = args
        here_bound = bounds[shard_pos]
        bucket_list = []
        for level_pos in range(LOGS):
            is_upper = jnp.bitwise_and(jnp.right_shift(shard_pos, level_pos), 1) == 1
            group_idx = jnp.right_shift(shard_pos, level_pos)
            start_row = jnp.left_shift(group_idx, level_pos)
            sibling = lax.dynamic_index_in_dim(group_levels[level_pos], jnp.maximum(group_idx - 1, 0), 0, keepdims=False)
            factor = jnp.repeat(jnp.exp(here_bound - bounds[start_row]), HEAD_DIM)[None, :]
            bucket_list.append(jnp.where(is_upper, factor * sibling.astype(jnp.float32), 0.0))
        buckets = jnp.stack(bucket_list)
        scores = jnp.dot(q_blk, k_blk.T, preferred_element_type=jnp.float32)
        c_heads = c_blk.T
        log_gaps = jnp.where(causal[None], c_heads[:, :, None] - c_heads[:, None, :], -jnp.inf)
        same_seg = s_blk[:, None] == s_blk[None, :]
        level_w = jnp.where(same_seg[None], w_blk[:, 0, :].T[:, :, None], w_blk[:, 1, :].T[:, :, None])
        weights_bf = (scores[None] * jnp.exp(log_gaps) * level_w).astype(jnp.bfloat16)
        v_heads = v_blk.reshape(TOK_DEV, HEAD_TOTAL, HEAD_DIM)
        local_out = jnp.einsum('htj,jhp->thp', weights_bf.astype(jnp.float32), v_heads.astype(jnp.float32), precision=highest)
        local_out = local_out.reshape(TOK_DEV, DI)
        level_reads = jnp.einsum('tn,lnc->tlc', q_blk.astype(jnp.float32), buckets, precision=highest)
        read_wts = jnp.repeat(w_blk[:, 2:, :], HEAD_DIM, axis=2)
        cross_out = lax.optimization_barrier(jnp.sum(level_reads * read_wts, axis=1)) * jnp.repeat(jnp.exp(c_blk), HEAD_DIM, axis=1)
        mixer_sum = local_out + cross_out + jnp.repeat(skip_gain, HEAD_DIM)[None, :] * v_blk.astype(jnp.float32)
        gated = mixer_sum * jax.nn.silu(z_blk.astype(jnp.float32))
        inv_rms = lax.rsqrt(lax.optimization_barrier(jnp.mean(gated * gated, axis=1, keepdims=True)) + epsilon)
        return (gated * inv_rms * norm_gain[None, :]).astype(jnp.bfloat16)
    hidden = lax.map(shard_out, (shard_ids, q_all, k_all, v_all, z_all, cum_all, level_wts, seg_all))
    hidden = hidden.reshape(TOKEN_TOTAL, DI)
    total_out = jnp.zeros((TOKEN_TOTAL, DM), jnp.float32)
    for group_pos in range(DI // GROUP_COLS):
        low_col = group_pos * GROUP_COLS
        partial_value = jnp.dot(hidden[:, low_col:low_col + GROUP_COLS], out_proj[low_col:low_col + GROUP_COLS], preferred_element_type=jnp.float32)
        total_out = total_out + lax.optimization_barrier(partial_value.astype(jnp.bfloat16)).astype(jnp.float32)
    return total_out.astype(jnp.bfloat16)
```

```python
import math

import jax
import jax.numpy as jnp
from jax import lax
from jax.sharding import PartitionSpec as P

epsilon = 1e-05
highest = lax.Precision.HIGHEST
f32 = jnp.float32
bf16 = jnp.bfloat16


def xor_permute(value, mask):
    pairs = [(source, source ^ mask) for source in range(lax.axis_size("seq"))]
    return lax.ppermute(value, "seq", pairs)


def widen(matrix, head_dim):
    return jnp.repeat(matrix, head_dim, axis=-1)


def per_device(
    queries,
    key_rows,
    values,
    gate_rows,
    log_decay,
    skip_gain,
    lam_index,
    segments,
    lam_table,
    norm_gain,
    out_proj,
):
    tok, state_dim = queries.shape
    head_count = log_decay.shape[1]
    cols = values.shape[1]
    head_dim = cols // head_count
    classes, level_count = lam_table.shape[:2]
    dev_count = lax.axis_size("seq")
    inner_total = cols * lax.axis_size("head")
    A = math.gcd(math.gcd(head_count, 8), dev_count)
    Z = dev_count // A
    a_bits = A.bit_length() - 1
    z_bits = Z.bit_length() - 1
    hg = head_count // A
    cg = hg * head_dim
    rows = A * tok
    out_cols = out_proj.shape[1]
    groups = [[z * A + i for i in range(A)] for z in range(Z)]
    me = lax.axis_index("seq")
    in_pos = lax.rem(me, A)
    z_pos = lax.div(me, A)

    def exchange(blocks):
        return lax.all_to_all(
            blocks, "seq", 0, 0, tiled=True, axis_index_groups=groups
        )

    def my_heads(array, width, axis):
        return lax.dynamic_slice_in_dim(array, in_pos * width, width, axis)

    w_blocks = out_proj.T.reshape(out_cols, A, cg).swapaxes(0, 1)
    w_block = exchange(w_blocks).reshape(A * out_cols, cg)

    shared = jnp.concatenate([queries, key_rows], axis=1)
    packed = jnp.concatenate(
        [
            values.reshape(tok, A, cg).swapaxes(0, 1),
            jnp.broadcast_to(shared[None], (A, tok, 2 * state_dim)),
        ],
        axis=2,
    )
    small = jnp.concatenate(
        [
            log_decay.reshape(tok, A, hg).swapaxes(0, 1),
            jnp.broadcast_to(lam_index.astype(f32)[None, :, None], (A, tok, 1)),
            jnp.broadcast_to(segments.astype(f32)[None, :, None], (A, tok, 1)),
        ],
        axis=2,
    )
    small = exchange(small)
    packed = exchange(packed)
    gates = exchange(gate_rows.reshape(tok, A, cg).swapaxes(0, 1))

    w_ring = [w_block]
    for _ in range(Z - 1):
        w_ring.append(
            lax.ppermute(
                w_ring[-1], "seq", [(s, (s + A) % dev_count) for s in range(dev_count)]
            )
        )

    x = packed[:, :, :cg]
    q = packed[:, :, cg : cg + state_dim]
    k = packed[:, :, cg + state_dim :]
    ld = small[:, :, :hg]
    lam = small[:, :, hg].reshape(rows).astype(jnp.int32)
    seg = small[:, :, hg + 1]

    cum = jnp.cumsum(ld, axis=1)
    span = cum[:, -1, :]
    onehot = (lam[:, None] == jnp.arange(classes, dtype=jnp.int32)[None, :]).astype(f32)
    table = my_heads(lam_table, hg, 2).reshape(classes, level_count * hg)
    lw = jnp.dot(onehot, table, precision=highest).reshape(A, tok, level_count, hg)

    decayed = (x.astype(f32) * widen(jnp.exp(span[:, None, :] - cum), head_dim)).astype(bf16)
    state = jnp.einsum("sjn,sjc->snc", k, decayed, preferred_element_type=f32).astype(bf16)

    cross = jnp.zeros((rows, cg), f32)
    total = span
    prefix = jnp.zeros((A, hg), f32)
    for b in range(a_bits):
        pairs = A >> (b + 1)
        lower, upper = state[0::2], state[1::2]
        low_total, up_total = total[0::2], total[1::2]
        wide = 2**b
        q_up = q.reshape(pairs, 2, wide * tok, state_dim)[:, 1]
        read = jnp.einsum("gtn,gnc->gtc", q_up, lower, preferred_element_type=f32)
        scale = (jnp.exp(cum + prefix[:, None, :]) * lw[:, :, 2 + b, :]).reshape(
            pairs, 2, wide * tok, hg
        )[:, 1]
        read = read * widen(scale, head_dim)
        cross = cross + jnp.stack([jnp.zeros_like(read), read], axis=1).reshape(rows, cg)
        factor = widen(jnp.exp(up_total), head_dim)[:, None, :]
        state = (upper.astype(f32) + factor * lower.astype(f32)).astype(bf16)
        is_up = jnp.arange(A, dtype=jnp.int32) // wide % 2 == 1
        low_rows = jnp.repeat(low_total, 2 * wide, axis=0)
        prefix = prefix + jnp.where(is_up[:, None], low_rows, 0.0)
        total = low_total + up_total
    state, total = state[0], total[0]
    q_rows = q.reshape(rows, state_dim)
    for zb in range(z_bits):
        other = xor_permute(state, A << zb)
        other_total = xor_permute(total[None, :], A << zb)[0]
        is_up = jnp.bitwise_and(jnp.right_shift(z_pos, zb), 1) == 1
        read = jnp.dot(q_rows, other, preferred_element_type=f32)
        scale = jnp.exp(cum + prefix[:, None, :]) * lw[:, :, 2 + a_bits + zb, :]
        scale = jnp.where(is_up, scale, 0.0).reshape(rows, hg)
        cross = cross + read * widen(scale, head_dim)
        if zb + 1 < z_bits:
            up_state = jnp.where(is_up, state, other).astype(f32)
            low_state = jnp.where(is_up, other, state).astype(f32)
            factor = widen(jnp.exp(jnp.where(is_up, total, other_total)), head_dim)
            state = (up_state + factor[None, :] * low_state).astype(bf16)
            prefix = prefix + jnp.where(is_up, other_total, 0.0)[None, :]
            total = total + other_total

    scores = jnp.einsum("stn,sjn->stj", q, k, preferred_element_type=f32)
    pos = jnp.arange(tok, dtype=jnp.int32)
    causal = pos[:, None] >= pos[None, :]
    cum_h = cum.swapaxes(1, 2)
    gaps = jnp.where(causal, cum_h[:, :, :, None] - cum_h[:, :, None, :], -jnp.inf)
    same = seg[:, :, None] == seg[:, None, :]
    lw0 = lw[:, :, 0, :].swapaxes(1, 2)[:, :, :, None]
    lw1 = lw[:, :, 1, :].swapaxes(1, 2)[:, :, :, None]
    weights = (
        scores[:, None] * jnp.exp(gaps) * jnp.where(same[:, None], lw0, lw1)
    ).astype(bf16)
    local = jnp.einsum(
        "shtj,sjhp->sthp",
        weights,
        x.reshape(A, tok, hg, head_dim),
        preferred_element_type=f32,
    ).reshape(rows, cg)

    skip = widen(my_heads(skip_gain, hg, 0), head_dim)[None, :]
    mixer = local + cross + skip * x.reshape(rows, cg).astype(f32)
    gated = mixer * jax.nn.silu(gates.reshape(rows, cg).astype(f32))
    squares = jnp.sum(gated * gated, axis=1)
    hidden = (gated * my_heads(norm_gain, cg, 0)[None, :]).astype(bf16)

    def reduce_group(part, order, narrow):
        left = list(range(a_bits))[::-1]
        part = part.reshape((2,) * a_bits + part.shape[1:])
        for b in order:
            axis = left.index(b)
            left.remove(b)
            bit = jnp.bitwise_and(jnp.right_shift(in_pos, b), 1)
            mine = lax.dynamic_index_in_dim(part, bit, axis, keepdims=False)
            theirs = lax.dynamic_index_in_dim(part, 1 - bit, axis, keepdims=False)
            part = mine + xor_permute(theirs.astype(narrow), 2**b).astype(f32)
        return part

    bits = list(range(a_bits))
    flipped = bits[:1] + bits[1:][::-1]
    square_sum = reduce_group(squares.reshape(A, tok), bits, f32)
    square_sum = lax.psum(square_sum, "head")
    inv_rms = lax.rsqrt(square_sum / inner_total + epsilon)[:, None]
    block_cols = A * out_cols
    out = jnp.zeros((tok, Z * block_cols), bf16)
    for step in range(Z):
        part = lax.dot_general(
            hidden, w_ring[step], (((1,), (1,)), ((), ())), preferred_element_type=f32
        )
        part = reduce_group(
            part.reshape(A, tok, block_cols), flipped if step % 2 else bits, bf16
        )
        block = lax.rem(z_pos - step + Z, Z)
        out = lax.dynamic_update_slice_in_dim(
            out, (part * inv_rms).astype(bf16), block * block_cols, 1
        )
    return lax.psum_scatter(out, "head", scatter_dimension=0, tiled=True)


def solution(mesh):
    return jax.shard_map(
        per_device,
        mesh=mesh,
        in_specs=(
            P("seq", None),
            P("seq", None),
            P("seq", "head"),
            P("seq", "head"),
            P("seq", "head"),
            P("head"),
            P("seq"),
            P("seq"),
            P(None, None, "head"),
            P("head"),
            P("head", "seq"),
        ),
        out_specs=P(("seq", "head"), None),
        check_vma=False,
    )
```

```python
import math

import jax
import jax.numpy as jnp
from jax import lax
from jax.experimental import pallas as pl
from jax.experimental.pallas import tpu as pltpu
from jax.sharding import PartitionSpec as P

epsilon = 1e-05
highest = lax.Precision.HIGHEST
f32 = jnp.float32
bf16 = jnp.bfloat16


def xor_permute(value, mask):
    pairs = [(source, source ^ mask) for source in range(lax.axis_size("seq"))]
    return lax.ppermute(value, "seq", pairs)


def widen(matrix, head_dim):
    return jnp.repeat(matrix, head_dim, axis=-1)


def spread(scale, expand):
    return jnp.dot(scale, expand, precision=highest, preferred_element_type=f32)


def state_kernel(bits, state_dim, packed_ref, scale_ref, up_ref, expand_ref, *outs):
    A = packed_ref.shape[0]
    expand = expand_ref[...]
    up_wide = spread(up_ref[...], expand)
    for s in range(A):
        decayed = packed_ref[s, :, 2 * state_dim :].astype(f32) * spread(scale_ref[s], expand)
        keys = packed_ref[s, :, state_dim : 2 * state_dim]
        outs[0][s] = lax.dot_general(
            keys,
            decayed.astype(bf16),
            (((0,), (0,)), ((), ())),
            preferred_element_type=f32,
        ).astype(bf16)
    row = 0
    for b in range(bits):
        for g in range(A >> (b + 1)):
            low = outs[b][2 * g].astype(f32)
            high = outs[b][2 * g + 1].astype(f32)
            merged = (high + up_wide[row : row + 1] * low).astype(bf16)
            if b + 1 < bits:
                outs[b + 1][g] = merged
            else:
                outs[b + 1][...] = merged
            row += 1


def state_call(packed, end_scale, up_rows, expand, *, state_dim, bits):
    A, _, width = packed.shape
    cg = width - 2 * state_dim
    shapes = [(A >> b, state_dim, cg) for b in range(bits)] + [(state_dim, cg)]
    vmem = pl.BlockSpec(memory_space=pltpu.VMEM)
    return pl.pallas_call(
        lambda *refs: state_kernel(bits, state_dim, *refs),
        out_shape=[jax.ShapeDtypeStruct(shape, bf16) for shape in shapes],
        in_specs=[vmem] * 4,
        out_specs=[vmem] * len(shapes),
        name="group_states",
        cost_estimate=pl.CostEstimate(
            flops=1 << 29, bytes_accessed=8 << 20, transcendentals=0
        ),
    )(packed, end_scale, up_rows, expand)


def local_kernel(
    state_dim, head_dim, bits, packed_ref, cum_ref, cum_t_ref, scale_ref, seg_ref,
    seg_t_ref, skip_ref, expand_ref, *rest
):
    states, out_ref = rest[:bits], rest[bits]
    tok, hg = cum_ref.shape[1:]
    cg = expand_ref.shape[1]
    q = packed_ref[0, :, :state_dim]
    keys = packed_ref[0, :, state_dim : 2 * state_dim]
    expand = expand_ref[...]
    scores = lax.dot_general(
        q, keys, (((1,), (1,)), ((), ())), preferred_element_type=f32
    )
    same = seg_ref[0] == seg_t_ref[0]
    t_pos = lax.broadcasted_iota(jnp.int32, (tok, tok), 0)
    j_pos = lax.broadcasted_iota(jnp.int32, (tok, tok), 1)
    causal = t_pos >= j_pos
    scales = scale_ref[0]
    cum = cum_ref[0]
    cum_t = cum_t_ref[0]
    x_wide = packed_ref[0, :, 2 * state_dim :]
    acc = skip_ref[...] * x_wide.astype(f32)
    for b in range(bits):
        read = jnp.dot(q, states[b][0], preferred_element_type=f32)
        acc = acc + read * spread(scales[:, (2 + b) * hg : (3 + b) * hg], expand)
    out_ref[...] = acc

    def head_weights(h):
        gaps = jnp.where(causal, cum[:, h : h + 1] - cum_t[h : h + 1, :], -jnp.inf)
        level_w = jnp.where(same, scales[:, h : h + 1], scales[:, hg + h : hg + h + 1])
        return (scores * jnp.exp(gaps) * level_w).astype(bf16)

    per_tile = max(1, 128 // head_dim)
    for first in range(0, hg, per_tile):
        heads = range(first, min(first + per_tile, hg))
        low, high = first * head_dim, min((first + per_tile) * head_dim, cg)
        x_tile = x_wide[:, low:high]
        lane_head = lax.broadcasted_iota(jnp.int32, (tok, high - low), 1) // head_dim
        tile = None
        for h in heads:
            part = jnp.dot(head_weights(h), x_tile, preferred_element_type=f32)
            tile = part if tile is None else jnp.where(lane_head == h - first, part, tile)
        out_ref[:, low:high] += tile


def local_call(
    packed, cum, cum_t, scales, seg, level_states, skip, expand, *, state_dim, head_dim
):
    A, tok, width = packed.shape
    cg = width - 2 * state_dim
    hg = cum.shape[2]
    bits = len(level_states)

    def shard_spec(*dims):
        return pl.BlockSpec((1,) + dims, lambda s: (s, 0, 0))

    def sibling_spec(b):
        return pl.BlockSpec(
            (1, state_dim, cg), lambda s: (jnp.maximum(s // 2**b - 1, 0), 0, 0)
        )

    def whole_spec(shape):
        return pl.BlockSpec(shape, lambda s: (0, 0))

    return pl.pallas_call(
        lambda *refs: local_kernel(state_dim, head_dim, bits, *refs),
        grid=(A,),
        out_shape=jax.ShapeDtypeStruct((A * tok, cg), f32),
        in_specs=[
            shard_spec(tok, width),
            shard_spec(tok, hg),
            shard_spec(hg, tok),
            shard_spec(tok, scales.shape[2]),
            shard_spec(tok, 1),
            shard_spec(1, tok),
            whole_spec((1, cg)),
            whole_spec(expand.shape),
        ]
        + [sibling_spec(b) for b in range(bits)],
        out_specs=pl.BlockSpec((tok, cg), lambda s: (s, 0)),
        name="local_mix",
        cost_estimate=pl.CostEstimate(
            flops=1 << 32, bytes_accessed=12 << 20, transcendentals=1 << 21
        ),
    )(packed, cum, cum_t, scales, seg[:, :, None], seg[:, None, :], skip, expand, *level_states)


def gate_kernel(levels, packed_ref, mixed_ref, scale_ref, gates_ref, gain_ref, expand_ref, *rest):
    others, (hidden_ref, square_ref) = rest[:levels], rest[levels:]
    hg = expand_ref.shape[0]
    q = packed_ref[0]
    expand = expand_ref[...]
    scales = scale_ref[0]
    acc = mixed_ref[...]
    for level in range(levels):
        read = jnp.dot(q, others[level][...], preferred_element_type=f32)
        acc = acc + read * spread(scales[:, level * hg : (level + 1) * hg], expand)
    gate = gates_ref[0].astype(f32)
    gated = acc * (gate / (1.0 + jnp.exp(-gate)))
    square_ref[0] = jnp.sum(gated * gated, axis=1, keepdims=True)
    hidden_ref[...] = (gated * gain_ref[...]).astype(bf16)


def gate_call(packed, mixed, others, other_scales, gates, gain, expand, *, state_dim):
    A, tok, cg = gates.shape
    levels = len(others)
    scales = jnp.concatenate(other_scales, axis=2)

    def shard_spec(*dims):
        return pl.BlockSpec((1,) + dims, lambda s: (s, 0, 0))

    def whole_spec(shape):
        return pl.BlockSpec(shape, lambda s: (0, 0))

    rows_spec = pl.BlockSpec((tok, cg), lambda s: (s, 0))
    return pl.pallas_call(
        lambda *refs: gate_kernel(levels, *refs),
        grid=(A,),
        out_shape=[
            jax.ShapeDtypeStruct((A * tok, cg), bf16),
            jax.ShapeDtypeStruct((A, tok, 1), f32),
        ],
        in_specs=[
            shard_spec(tok, state_dim),
            rows_spec,
            shard_spec(tok, scales.shape[2]),
            shard_spec(tok, cg),
            whole_spec((1, cg)),
            whole_spec(expand.shape),
        ]
        + [whole_spec((state_dim, cg))] * levels,
        out_specs=[rows_spec, shard_spec(tok, 1)],
        name="gate_mix",
        cost_estimate=pl.CostEstimate(
            flops=1 << 30, bytes_accessed=8 << 20, transcendentals=1 << 20
        ),
    )(packed, mixed, scales, gates, gain, expand, *others)


def per_device(
    queries,
    key_rows,
    values,
    gate_rows,
    log_decay,
    skip_gain,
    lam_index,
    segments,
    lam_table,
    norm_gain,
    out_proj,
):
    tok, state_dim = queries.shape
    head_count = log_decay.shape[1]
    cols = values.shape[1]
    head_dim = cols // head_count
    classes, level_count = lam_table.shape[:2]
    dev_count = lax.axis_size("seq")
    inner_total = cols * lax.axis_size("head")
    A = math.gcd(math.gcd(head_count, 8), dev_count)
    Z = dev_count // A
    a_bits = A.bit_length() - 1
    z_bits = Z.bit_length() - 1
    hg = head_count // A
    cg = hg * head_dim
    rows = A * tok
    out_cols = out_proj.shape[1]
    groups = [[z * A + i for i in range(A)] for z in range(Z)]
    me = lax.axis_index("seq")
    in_pos = lax.rem(me, A)
    z_pos = lax.div(me, A)

    def exchange(blocks):
        return lax.all_to_all(
            blocks, "seq", 0, 0, tiled=True, axis_index_groups=groups
        )

    def my_heads(array, width, axis):
        return lax.dynamic_slice_in_dim(array, in_pos * width, width, axis)

    w_blocks = out_proj.T.reshape(out_cols, A, cg).swapaxes(0, 1)
    w_block = exchange(w_blocks).reshape(A * out_cols, cg)

    cum_own = jnp.cumsum(log_decay, axis=0)
    shared = jnp.concatenate([queries, key_rows], axis=1)
    packed = jnp.concatenate(
        [
            jnp.broadcast_to(shared[None], (A, tok, 2 * state_dim)),
            values.reshape(tok, A, cg).swapaxes(0, 1),
        ],
        axis=2,
    )
    small = jnp.concatenate(
        [
            cum_own.reshape(tok, A, hg).swapaxes(0, 1),
            jnp.broadcast_to(lam_index.astype(f32)[None, :, None], (A, tok, 1)),
            jnp.broadcast_to(segments.astype(f32)[None, :, None], (A, tok, 1)),
        ],
        axis=2,
    )
    small = exchange(small)
    packed = exchange(packed)
    gates = exchange(gate_rows.reshape(tok, A, cg).swapaxes(0, 1))

    w_ring = [w_block]
    for _ in range(Z - 1):
        w_ring.append(
            lax.ppermute(
                w_ring[-1], "seq", [(s, (s + A) % dev_count) for s in range(dev_count)]
            )
        )

    cum = small[:, :, :hg]
    lam = small[:, :, hg].reshape(rows).astype(jnp.int32)
    seg = small[:, :, hg + 1]
    span = cum[:, -1, :]
    onehot = (lam[:, None] == jnp.arange(classes, dtype=jnp.int32)[None, :]).astype(f32)
    table = my_heads(lam_table, hg, 2).reshape(classes, level_count * hg)
    lw = jnp.dot(onehot, table, precision=highest).reshape(A, tok, level_count * hg)
    expand = (
        jnp.arange(hg, dtype=jnp.int32)[:, None]
        == jnp.arange(cg, dtype=jnp.int32)[None, :] // head_dim
    ).astype(f32)

    total = span
    prefix = jnp.zeros((A, hg), f32)
    prefixes = []
    up_factors = []
    for b in range(a_bits):
        wide = 2**b
        low_total, up_total = total[0::2], total[1::2]
        is_up = (jnp.arange(A, dtype=jnp.int32) // wide % 2 == 1)[:, None]
        prefixes.append(jnp.where(is_up, prefix, -jnp.inf))
        up_factors.append(jnp.exp(up_total))
        prefix = prefix + jnp.where(is_up, jnp.repeat(low_total, 2 * wide, axis=0), 0.0)
        total = low_total + up_total
    total = total[0]

    def level_scale(before, level):
        weight = lw[:, :, (2 + level) * hg : (3 + level) * hg]
        return jnp.exp(cum + before[:, None, :]) * weight

    end_scale = jnp.exp(span[:, None, :] - cum)
    up_rows = jnp.concatenate(up_factors, axis=0)
    *level_states, state = state_call(
        packed, end_scale, up_rows, expand, state_dim=state_dim, bits=a_bits
    )
    local_scales = [lw[:, :, : 2 * hg]]
    local_scales += [level_scale(before, b) for b, before in enumerate(prefixes)]
    local_scales = jnp.concatenate(local_scales, axis=2)

    others, other_scales = [], []
    for zb in range(z_bits):
        other = xor_permute(state, A << zb)
        other_total = xor_permute(total[None, :], A << zb)[0]
        is_up = jnp.bitwise_and(jnp.right_shift(z_pos, zb), 1) == 1
        others.append(other)
        before = jnp.where(is_up, prefix, -jnp.inf)
        other_scales.append(level_scale(before, a_bits + zb))
        if zb + 1 < z_bits:
            up_state = jnp.where(is_up, state, other).astype(f32)
            low_state = jnp.where(is_up, other, state).astype(f32)
            factor = widen(jnp.exp(jnp.where(is_up, total, other_total)), head_dim)
            state = (up_state + factor[None, :] * low_state).astype(bf16)
            prefix = prefix + jnp.where(is_up, other_total, 0.0)[None, :]
            total = total + other_total

    skip = widen(my_heads(skip_gain, hg, 0), head_dim)[None, :]
    mixed = local_call(
        packed, cum, cum.swapaxes(1, 2), local_scales, seg, level_states, skip, expand,
        state_dim=state_dim, head_dim=head_dim,
    )
    gain = my_heads(norm_gain, cg, 0)[None, :]
    hidden, squares = gate_call(
        packed, mixed, others, other_scales, gates, gain, expand, state_dim=state_dim
    )

    def reduce_group(part, order, narrow):
        left = list(range(a_bits))[::-1]
        part = part.reshape((2,) * a_bits + part.shape[1:])
        for b in order:
            axis = left.index(b)
            left.remove(b)
            bit = jnp.bitwise_and(jnp.right_shift(in_pos, b), 1)
            mine = lax.dynamic_index_in_dim(part, bit, axis, keepdims=False)
            theirs = lax.dynamic_index_in_dim(part, 1 - bit, axis, keepdims=False)
            part = mine + xor_permute(theirs.astype(narrow), 2**b).astype(f32)
        return part

    bits = list(range(a_bits))
    flipped = bits[:1] + bits[1:][::-1]
    square_sum = reduce_group(squares.reshape(A, tok), bits, f32)
    square_sum = lax.psum(square_sum, "head")
    inv_rms = lax.rsqrt(square_sum / inner_total + epsilon)[:, None]
    block_cols = A * out_cols
    out = jnp.zeros((tok, Z * block_cols), bf16)
    for step in range(Z):
        part = lax.dot_general(
            hidden, w_ring[step], (((1,), (1,)), ((), ())), preferred_element_type=f32
        )
        part = reduce_group(
            part.reshape(A, tok, block_cols), flipped if step % 2 else bits, bf16
        )
        block = lax.rem(z_pos - step + Z, Z)
        out = lax.dynamic_update_slice_in_dim(
            out, (part * inv_rms).astype(bf16), block * block_cols, 1
        )
    return lax.psum_scatter(out, "head", scatter_dimension=0, tiled=True)


def solution(mesh):
    return jax.shard_map(
        per_device,
        mesh=mesh,
        in_specs=(
            P("seq", None),
            P("seq", None),
            P("seq", "head"),
            P("seq", "head"),
            P("seq", "head"),
            P("head"),
            P("seq"),
            P("seq"),
            P(None, None, "head"),
            P("head"),
            P("head", "seq"),
        ),
        out_specs=P(("seq", "head"), None),
        check_vma=False,
    )
```

```python
import math

import jax
import jax.numpy as jnp
from jax import lax
from jax.experimental import pallas as pl
from jax.experimental.pallas import tpu as pltpu
from jax.sharding import PartitionSpec as P

epsilon = 1e-05
highest = lax.Precision.HIGHEST
f32 = jnp.float32
bf16 = jnp.bfloat16


def xor_permute(value, mask):
    pairs = [(source, source ^ mask) for source in range(lax.axis_size("seq"))]
    return lax.ppermute(value, "seq", pairs)


def widen(matrix, head_dim):
    return jnp.repeat(matrix, head_dim, axis=-1)


def pack_kernel(groups, q_ref, k_ref, x_ref, decay_ref, lam_ref, seg_ref, out_ref):
    tok, state_dim = q_ref.shape
    cg = x_ref.shape[1] // groups
    hg = decay_ref.shape[1] // groups
    t_pos = lax.broadcasted_iota(jnp.int32, (tok, tok), 0)
    j_pos = lax.broadcasted_iota(jnp.int32, (tok, tok), 1)
    ones = jnp.where(t_pos >= j_pos, 1.0, 0.0).astype(f32)
    cum = jnp.dot(ones, decay_ref[...], precision=highest, preferred_element_type=f32)
    first = cum.astype(bf16).astype(f32)
    second = (cum - first).astype(bf16).astype(f32)
    third = cum - first - second
    pad = out_ref.shape[2] - 2 * state_dim - cg - 3 * hg - 2
    tail = [lam_ref[...], seg_ref[...], jnp.zeros((tok, pad), f32)]
    for s in range(groups):
        out_ref[s, :, :state_dim] = q_ref[...]
        out_ref[s, :, state_dim : 2 * state_dim] = k_ref[...]
        out_ref[s, :, 2 * state_dim : 2 * state_dim + cg] = x_ref[:, s * cg : (s + 1) * cg]
        parts = [part[:, s * hg : (s + 1) * hg] for part in (first, second, third)]
        small = jnp.concatenate(parts + tail, axis=1)
        out_ref[s, :, 2 * state_dim + cg :] = small.astype(bf16)


def pack_call(queries, key_rows, values, log_decay, lam, seg, *, groups):
    tok, state_dim = queries.shape
    width = 2 * state_dim + values.shape[1] // groups + 3 * (log_decay.shape[1] // groups) + 2
    vmem = pl.BlockSpec(memory_space=pltpu.VMEM)
    return pl.pallas_call(
        lambda *refs: pack_kernel(groups, *refs),
        out_shape=jax.ShapeDtypeStruct((groups, tok, pl.cdiv(width + 1, 128) * 128), bf16),
        in_specs=[vmem] * 6,
        out_specs=vmem,
        name="pack",
        cost_estimate=pl.CostEstimate(
            flops=1 << 22, bytes_accessed=4 << 20, transcendentals=0
        ),
    )(queries, key_rows, values, log_decay, lam, seg)


def spread(scale, expand):
    high = scale.astype(bf16)
    low = (scale - high.astype(f32)).astype(bf16)
    return jnp.dot(high, expand, preferred_element_type=f32) + jnp.dot(
        low, expand, preferred_element_type=f32
    )


def state_kernel(bits, state_dim, packed_ref, scale_ref, up_ref, expand_ref, *outs):
    A = packed_ref.shape[0]
    expand = expand_ref[...]
    up_wide = spread(up_ref[...], expand)
    for s in range(A):
        decayed = packed_ref[s, :, 2 * state_dim : 2 * state_dim + expand.shape[1]].astype(f32) * spread(scale_ref[s], expand)
        keys = packed_ref[s, :, state_dim : 2 * state_dim]
        outs[0][s] = lax.dot_general(
            keys,
            decayed.astype(bf16),
            (((0,), (0,)), ((), ())),
            preferred_element_type=f32,
        ).astype(bf16)
    row = 0
    for b in range(bits):
        for g in range(A >> (b + 1)):
            low = outs[b][2 * g].astype(f32)
            high = outs[b][2 * g + 1].astype(f32)
            merged = (high + up_wide[row : row + 1] * low).astype(bf16)
            if b + 1 < bits:
                outs[b + 1][g] = merged
            else:
                outs[b + 1][...] = merged
            row += 1


def state_call(packed, end_scale, up_rows, expand, *, state_dim, bits):
    A = packed.shape[0]
    cg = expand.shape[1]
    shapes = [(A >> b, state_dim, cg) for b in range(bits)] + [(state_dim, cg)]
    vmem = pl.BlockSpec(memory_space=pltpu.VMEM)
    return pl.pallas_call(
        lambda *refs: state_kernel(bits, state_dim, *refs),
        out_shape=[jax.ShapeDtypeStruct(shape, bf16) for shape in shapes],
        in_specs=[vmem] * 4,
        out_specs=[vmem] * len(shapes),
        name="group_states",
        cost_estimate=pl.CostEstimate(
            flops=1 << 29, bytes_accessed=8 << 20, transcendentals=0
        ),
    )(packed, end_scale, up_rows, expand)


def local_kernel(
    state_dim, head_dim, bits, packed_ref, cum_ref, cum_t_ref, scale_ref, seg_ref,
    seg_t_ref, skip_ref, expand_ref, *rest
):
    states, out_ref = rest[:bits], rest[bits]
    tok, hg = cum_ref.shape[1:]
    cg = expand_ref.shape[1]
    q = packed_ref[0, :, :state_dim]
    keys = packed_ref[0, :, state_dim : 2 * state_dim]
    expand = expand_ref[...]
    scores = lax.dot_general(
        q, keys, (((1,), (1,)), ((), ())), preferred_element_type=f32
    )
    same = seg_ref[0] == seg_t_ref[0]
    t_pos = lax.broadcasted_iota(jnp.int32, (tok, tok), 0)
    j_pos = lax.broadcasted_iota(jnp.int32, (tok, tok), 1)
    causal = t_pos >= j_pos
    scales = scale_ref[0]
    cum = cum_ref[0]
    cum_t = cum_t_ref[0]
    x_wide = packed_ref[0, :, 2 * state_dim : 2 * state_dim + cg]
    acc = skip_ref[...] * x_wide.astype(f32)
    for b in range(bits):
        read = jnp.dot(q, states[b][0], preferred_element_type=f32)
        acc = acc + read * spread(scales[:, (2 + b) * hg : (3 + b) * hg], expand)
    out_ref[...] = acc

    def head_weights(h):
        gaps = jnp.where(causal, cum[:, h : h + 1] - cum_t[h : h + 1, :], -jnp.inf)
        level_w = jnp.where(same, scales[:, h : h + 1], scales[:, hg + h : hg + h + 1])
        return (scores * jnp.exp(gaps) * level_w).astype(bf16)

    per_tile = max(1, 128 // head_dim)
    for first in range(0, hg, per_tile):
        heads = range(first, min(first + per_tile, hg))
        low, high = first * head_dim, min((first + per_tile) * head_dim, cg)
        x_tile = x_wide[:, low:high]
        lane_head = lax.broadcasted_iota(jnp.int32, (tok, high - low), 1) // head_dim
        tile = None
        for h in heads:
            part = jnp.dot(head_weights(h), x_tile, preferred_element_type=f32)
            tile = part if tile is None else jnp.where(lane_head == h - first, part, tile)
        out_ref[:, low:high] += tile


def local_call(
    packed, cum, cum_t, scales, seg, level_states, skip, expand, *, state_dim, head_dim
):
    A, tok, width = packed.shape
    cg = expand.shape[1]
    hg = cum.shape[2]
    bits = len(level_states)

    def shard_spec(*dims):
        return pl.BlockSpec((1,) + dims, lambda s: (s, 0, 0))

    def sibling_spec(b):
        return pl.BlockSpec(
            (1, state_dim, cg), lambda s: (jnp.maximum(s // 2**b - 1, 0), 0, 0)
        )

    def whole_spec(shape):
        return pl.BlockSpec(shape, lambda s: (0, 0))

    return pl.pallas_call(
        lambda *refs: local_kernel(state_dim, head_dim, bits, *refs),
        grid=(A,),
        out_shape=jax.ShapeDtypeStruct((A * tok, cg), f32),
        in_specs=[
            shard_spec(tok, width),
            shard_spec(tok, hg),
            shard_spec(hg, tok),
            shard_spec(tok, scales.shape[2]),
            shard_spec(tok, 1),
            shard_spec(1, tok),
            whole_spec((1, cg)),
            whole_spec(expand.shape),
        ]
        + [sibling_spec(b) for b in range(bits)],
        out_specs=pl.BlockSpec((tok, cg), lambda s: (s, 0)),
        name="local_mix",
        cost_estimate=pl.CostEstimate(
            flops=1 << 32, bytes_accessed=12 << 20, transcendentals=1 << 21
        ),
    )(packed, cum, cum_t, scales, seg[:, :, None], seg[:, None, :], skip, expand, *level_states)


def gate_kernel(levels, packed_ref, mixed_ref, scale_ref, gates_ref, gain_ref, expand_ref, *rest):
    others, (hidden_ref, square_ref) = rest[:levels], rest[levels:]
    hg = expand_ref.shape[0]
    q = packed_ref[0]
    expand = expand_ref[...]
    scales = scale_ref[0]
    acc = mixed_ref[...]
    for level in range(levels):
        read = jnp.dot(q, others[level][...], preferred_element_type=f32)
        acc = acc + read * spread(scales[:, level * hg : (level + 1) * hg], expand)
    gate = gates_ref[0].astype(f32)
    gated = acc * (gate / (1.0 + jnp.exp(-gate)))
    square_ref[0] = jnp.sum(gated * gated, axis=1, keepdims=True)
    hidden_ref[...] = (gated * gain_ref[...]).astype(bf16)


def gate_call(packed, mixed, others, other_scales, gates, gain, expand, *, state_dim):
    A, tok, cg = gates.shape
    levels = len(others)
    scales = jnp.concatenate(other_scales, axis=2)

    def shard_spec(*dims):
        return pl.BlockSpec((1,) + dims, lambda s: (s, 0, 0))

    def whole_spec(shape):
        return pl.BlockSpec(shape, lambda s: (0, 0))

    rows_spec = pl.BlockSpec((tok, cg), lambda s: (s, 0))
    return pl.pallas_call(
        lambda *refs: gate_kernel(levels, *refs),
        grid=(A,),
        out_shape=[
            jax.ShapeDtypeStruct((A * tok, cg), bf16),
            jax.ShapeDtypeStruct((A, tok, 1), f32),
        ],
        in_specs=[
            shard_spec(tok, state_dim),
            rows_spec,
            shard_spec(tok, scales.shape[2]),
            shard_spec(tok, cg),
            whole_spec((1, cg)),
            whole_spec(expand.shape),
        ]
        + [whole_spec((state_dim, cg))] * levels,
        out_specs=[rows_spec, shard_spec(tok, 1)],
        name="gate_mix",
        cost_estimate=pl.CostEstimate(
            flops=1 << 30, bytes_accessed=8 << 20, transcendentals=1 << 20
        ),
    )(packed, mixed, scales, gates, gain, expand, *others)


def per_device(
    queries,
    key_rows,
    values,
    gate_rows,
    log_decay,
    skip_gain,
    lam_index,
    segments,
    lam_table,
    norm_gain,
    out_proj,
):
    tok, state_dim = queries.shape
    head_count = log_decay.shape[1]
    cols = values.shape[1]
    head_dim = cols // head_count
    classes, level_count = lam_table.shape[:2]
    dev_count = lax.axis_size("seq")
    inner_total = cols * lax.axis_size("head")
    A = math.gcd(math.gcd(head_count, 8), dev_count)
    Z = dev_count // A
    a_bits = A.bit_length() - 1
    z_bits = Z.bit_length() - 1
    hg = head_count // A
    cg = hg * head_dim
    rows = A * tok
    out_cols = out_proj.shape[1]
    groups = [[z * A + i for i in range(A)] for z in range(Z)]
    me = lax.axis_index("seq")
    in_pos = lax.rem(me, A)
    z_pos = lax.div(me, A)

    def exchange(blocks):
        return lax.all_to_all(
            blocks, "seq", 0, 0, tiled=True, axis_index_groups=groups
        )

    def my_heads(array, width, axis):
        return lax.dynamic_slice_in_dim(array, in_pos * width, width, axis)

    w_blocks = out_proj.T.reshape(out_cols, A, cg).swapaxes(0, 1)
    w_block = exchange(w_blocks).reshape(A * out_cols, cg)

    packed = pack_call(
        queries,
        key_rows,
        values,
        log_decay,
        lam_index.astype(f32)[:, None],
        segments.astype(f32)[:, None],
        groups=A,
    )
    packed = exchange(packed)
    small = packed[:, :, 2 * state_dim + cg :].astype(f32)

    def shift(block, step):
        pairs = [(p, (p + step * A) % dev_count) for p in range(dev_count)]
        return lax.ppermute(block, "seq", pairs)

    w_ring = [(0, w_block)]
    above = below = w_block
    if Z > 1:
        above = shift(w_block, 1)
        w_ring.append((1, above))
    if Z > 2:
        below = shift(w_block, -1)
        w_ring.append((-1, below))

    cum = small[:, :, :hg] + small[:, :, hg : 2 * hg] + small[:, :, 2 * hg : 3 * hg]
    lam = small[:, :, 3 * hg].reshape(rows).astype(jnp.int32)
    seg = small[:, :, 3 * hg + 1]
    span = cum[:, -1, :]
    onehot = (lam[:, None] == jnp.arange(classes, dtype=jnp.int32)[None, :]).astype(f32)
    table = my_heads(lam_table, hg, 2).reshape(classes, level_count * hg)
    lw = jnp.dot(onehot, table, precision=highest).reshape(A, tok, level_count * hg)
    expand = (
        jnp.arange(hg, dtype=jnp.int32)[:, None]
        == jnp.arange(cg, dtype=jnp.int32)[None, :] // head_dim
    ).astype(bf16)

    total = span
    prefix = jnp.zeros((A, hg), f32)
    prefixes = []
    up_factors = []
    for b in range(a_bits):
        wide = 2**b
        low_total, up_total = total[0::2], total[1::2]
        is_up = (jnp.arange(A, dtype=jnp.int32) // wide % 2 == 1)[:, None]
        prefixes.append(jnp.where(is_up, prefix, -jnp.inf))
        up_factors.append(jnp.exp(up_total))
        prefix = prefix + jnp.where(is_up, jnp.repeat(low_total, 2 * wide, axis=0), 0.0)
        total = low_total + up_total
    total = total[0]

    def level_scale(before, level):
        weight = lw[:, :, (2 + level) * hg : (3 + level) * hg]
        return jnp.exp(cum + before[:, None, :]) * weight

    end_scale = jnp.exp(span[:, None, :] - cum)
    up_rows = jnp.concatenate(up_factors, axis=0)
    *level_states, state = state_call(
        packed, end_scale, up_rows, expand, state_dim=state_dim, bits=a_bits
    )
    gate_blocks = gate_rows.reshape(tok, A, cg).swapaxes(0, 1)
    gate_blocks, state, total = lax.optimization_barrier((gate_blocks, state, total))
    gates = exchange(gate_blocks)
    local_scales = [lw[:, :, : 2 * hg]]
    local_scales += [level_scale(before, b) for b, before in enumerate(prefixes)]
    local_scales = jnp.concatenate(local_scales, axis=2)

    others, other_scales = [], []
    for zb in range(z_bits):
        other = xor_permute(state, A << zb)
        other_total = xor_permute(total[None, :], A << zb)[0]
        is_up = jnp.bitwise_and(jnp.right_shift(z_pos, zb), 1) == 1
        others.append(other)
        before = jnp.where(is_up, prefix, -jnp.inf)
        other_scales.append(level_scale(before, a_bits + zb))
        if zb + 1 < z_bits:
            up_state = jnp.where(is_up, state, other).astype(f32)
            low_state = jnp.where(is_up, other, state).astype(f32)
            factor = widen(jnp.exp(jnp.where(is_up, total, other_total)), head_dim)
            state = (up_state + factor[None, :] * low_state).astype(bf16)
            prefix = prefix + jnp.where(is_up, other_total, 0.0)[None, :]
            total = total + other_total

    for distance in range(2, Z // 2 + 1):
        above, others = lax.optimization_barrier((above, others))
        above = shift(above, 1)
        w_ring.append((distance, above))
        if 2 * distance < Z:
            below = shift(below, -1)
            w_ring.append((-distance, below))

    skip = widen(my_heads(skip_gain, hg, 0), head_dim)[None, :]
    mixed = local_call(
        packed, cum, cum.swapaxes(1, 2), local_scales, seg, level_states, skip, expand,
        state_dim=state_dim, head_dim=head_dim,
    )
    gain = my_heads(norm_gain, cg, 0)[None, :]
    hidden, squares = gate_call(
        packed, mixed, others, other_scales, gates, gain, expand, state_dim=state_dim
    )

    def reduce_group(part, order, narrow):
        left = list(range(a_bits))[::-1]
        part = part.reshape((2,) * a_bits + part.shape[1:])
        for b in order:
            axis = left.index(b)
            left.remove(b)
            bit = jnp.bitwise_and(jnp.right_shift(in_pos, b), 1)
            mine = lax.dynamic_index_in_dim(part, bit, axis, keepdims=False)
            theirs = lax.dynamic_index_in_dim(part, 1 - bit, axis, keepdims=False)
            part = mine + xor_permute(theirs.astype(narrow), 2**b).astype(f32)
        return part

    bits = list(range(a_bits))
    flipped = bits[:1] + bits[1:][::-1]
    square_sum = reduce_group(squares.reshape(A, tok), bits, f32)
    square_sum = lax.psum(square_sum, "head")
    inv_rms = lax.rsqrt(square_sum / inner_total + epsilon)[:, None]
    block_cols = A * out_cols
    out = jnp.zeros((tok, Z * block_cols), bf16)
    for step, (distance, w_part) in enumerate(w_ring):
        part = lax.dot_general(
            hidden, w_part, (((1,), (1,)), ((), ())), preferred_element_type=f32
        )
        part = reduce_group(
            part.reshape(A, tok, block_cols), flipped if step % 2 else bits, bf16
        )
        block = lax.rem(z_pos - distance + Z, Z)
        out = lax.dynamic_update_slice_in_dim(
            out, (part * inv_rms).astype(bf16), block * block_cols, 1
        )
    return lax.psum_scatter(out, "head", scatter_dimension=0, tiled=True)


def solution(mesh):
    return jax.shard_map(
        per_device,
        mesh=mesh,
        in_specs=(
            P("seq", None),
            P("seq", None),
            P("seq", "head"),
            P("seq", "head"),
            P("seq", "head"),
            P("head"),
            P("seq"),
            P("seq"),
            P(None, None, "head"),
            P("head"),
            P("head", "seq"),
        ),
        out_specs=P(("seq", "head"), None),
        check_vma=False,
    )
```

```python
import math

import jax
import jax.numpy as jnp
from jax import lax
from jax.experimental import pallas as pl
from jax.experimental.pallas import tpu as pltpu
from jax.sharding import PartitionSpec as P

epsilon = 1e-05
highest = lax.Precision.HIGHEST
f32 = jnp.float32
bf16 = jnp.bfloat16


def xor_permute(value, mask):
    pairs = [(source, source ^ mask) for source in range(lax.axis_size("seq"))]
    return lax.ppermute(value, "seq", pairs)


def widen(matrix, head_dim):
    return jnp.repeat(matrix, head_dim, axis=-1)


def pack_kernel(groups, q_ref, k_ref, x_ref, decay_ref, lam_ref, seg_ref, out_ref):
    tok, state_dim = q_ref.shape
    cg = x_ref.shape[1] // groups
    hg = decay_ref.shape[1] // groups
    t_pos = lax.broadcasted_iota(jnp.int32, (tok, tok), 0)
    j_pos = lax.broadcasted_iota(jnp.int32, (tok, tok), 1)
    ones = jnp.where(t_pos >= j_pos, 1.0, 0.0).astype(f32)
    cum = jnp.dot(ones, decay_ref[...], precision=highest, preferred_element_type=f32)
    first = cum.astype(bf16).astype(f32)
    second = (cum - first).astype(bf16).astype(f32)
    third = cum - first - second
    pad = out_ref.shape[2] - 2 * state_dim - cg - 3 * hg - 2
    tail = [lam_ref[...], seg_ref[...], jnp.zeros((tok, pad), f32)]
    for s in range(groups):
        out_ref[s, :, :state_dim] = q_ref[...]
        out_ref[s, :, state_dim : 2 * state_dim] = k_ref[...]
        out_ref[s, :, 2 * state_dim : 2 * state_dim + cg] = x_ref[:, s * cg : (s + 1) * cg]
        parts = [part[:, s * hg : (s + 1) * hg] for part in (first, second, third)]
        small = jnp.concatenate(parts + tail, axis=1)
        out_ref[s, :, 2 * state_dim + cg :] = small.astype(bf16)


def pack_call(queries, key_rows, values, log_decay, lam, seg, *, groups):
    tok, state_dim = queries.shape
    width = 2 * state_dim + values.shape[1] // groups + 3 * (log_decay.shape[1] // groups) + 2
    vmem = pl.BlockSpec(memory_space=pltpu.VMEM)
    return pl.pallas_call(
        lambda *refs: pack_kernel(groups, *refs),
        out_shape=jax.ShapeDtypeStruct((groups, tok, pl.cdiv(width + 1, 128) * 128), bf16),
        in_specs=[vmem] * 6,
        out_specs=vmem,
        name="pack",
        cost_estimate=pl.CostEstimate(
            flops=1 << 22, bytes_accessed=4 << 20, transcendentals=0
        ),
    )(queries, key_rows, values, log_decay, lam, seg)


def spread(scale, expand):
    high = scale.astype(bf16)
    low = (scale - high.astype(f32)).astype(bf16)
    return jnp.dot(high, expand, preferred_element_type=f32) + jnp.dot(
        low, expand, preferred_element_type=f32
    )


def state_kernel(bits, state_dim, packed_ref, expand_ref, *outs):
    A = packed_ref.shape[0]
    hg, cg = expand_ref.shape
    expand = expand_ref[...]
    totals = []
    for s in range(A):
        tail = packed_ref[s, :, 2 * state_dim + cg :].astype(f32)
        cum = tail[:, :hg] + tail[:, hg : 2 * hg] + tail[:, 2 * hg : 3 * hg]
        last = cum[-1:, :]
        totals.append(last)
        decayed = packed_ref[s, :, 2 * state_dim : 2 * state_dim + cg].astype(f32) * spread(
            jnp.exp(last - cum), expand
        )
        keys = packed_ref[s, :, state_dim : 2 * state_dim]
        outs[0][s] = lax.dot_general(
            keys,
            decayed.astype(bf16),
            (((0,), (0,)), ((), ())),
            preferred_element_type=f32,
        ).astype(bf16)
    for b in range(bits):
        up_wide = [
            spread(jnp.exp(jnp.broadcast_to(totals[2 * g + 1], (8, hg))), expand)[:1]
            for g in range(A >> (b + 1))
        ]
        for g in range(A >> (b + 1)):
            low = outs[b][2 * g].astype(f32)
            high = outs[b][2 * g + 1].astype(f32)
            merged = (high + up_wide[g] * low).astype(bf16)
            if b + 1 < bits:
                outs[b + 1][g] = merged
            else:
                outs[b + 1][...] = merged
        totals = [totals[2 * g] + totals[2 * g + 1] for g in range(A >> (b + 1))]


def state_call(packed, expand, *, state_dim, bits):
    A = packed.shape[0]
    cg = expand.shape[1]
    shapes = [(A >> b, state_dim, cg) for b in range(bits)] + [(state_dim, cg)]
    vmem = pl.BlockSpec(memory_space=pltpu.VMEM)
    return pl.pallas_call(
        lambda *refs: state_kernel(bits, state_dim, *refs),
        out_shape=[jax.ShapeDtypeStruct(shape, bf16) for shape in shapes],
        in_specs=[vmem] * 2,
        out_specs=[vmem] * len(shapes),
        name="group_states",
        cost_estimate=pl.CostEstimate(
            flops=1 << 29, bytes_accessed=8 << 20, transcendentals=0
        ),
    )(packed, expand)


def local_kernel(
    state_dim, head_dim, bits, packed_ref, cum_ref, cum_t_ref, scale_ref, seg_ref,
    seg_t_ref, skip_ref, expand_ref, *rest
):
    states, out_ref = rest[:bits], rest[bits]
    tok, hg = cum_ref.shape[1:]
    cg = expand_ref.shape[1]
    q = packed_ref[0, :, :state_dim]
    keys = packed_ref[0, :, state_dim : 2 * state_dim]
    expand = expand_ref[...]
    scores = lax.dot_general(
        q, keys, (((1,), (1,)), ((), ())), preferred_element_type=f32
    )
    same = seg_ref[0] == seg_t_ref[0]
    t_pos = lax.broadcasted_iota(jnp.int32, (tok, tok), 0)
    j_pos = lax.broadcasted_iota(jnp.int32, (tok, tok), 1)
    causal = t_pos >= j_pos
    scales = scale_ref[0]
    cum = cum_ref[0]
    cum_t = cum_t_ref[0]
    x_wide = packed_ref[0, :, 2 * state_dim : 2 * state_dim + cg]
    acc = skip_ref[...] * x_wide.astype(f32)
    for b in range(bits):
        read = jnp.dot(q, states[b][0], preferred_element_type=f32)
        acc = acc + read * spread(scales[:, (2 + b) * hg : (3 + b) * hg], expand)
    out_ref[...] = acc

    def head_weights(h):
        gaps = jnp.where(causal, cum[:, h : h + 1] - cum_t[h : h + 1, :], -jnp.inf)
        level_w = jnp.where(same, scales[:, h : h + 1], scales[:, hg + h : hg + h + 1])
        return (scores * jnp.exp(gaps) * level_w).astype(bf16)

    per_tile = max(1, 128 // head_dim)
    for first in range(0, hg, per_tile):
        heads = range(first, min(first + per_tile, hg))
        low, high = first * head_dim, min((first + per_tile) * head_dim, cg)
        x_tile = x_wide[:, low:high]
        lane_head = lax.broadcasted_iota(jnp.int32, (tok, high - low), 1) // head_dim
        tile = None
        for h in heads:
            part = jnp.dot(head_weights(h), x_tile, preferred_element_type=f32)
            tile = part if tile is None else jnp.where(lane_head == h - first, part, tile)
        out_ref[:, low:high] += tile


def local_call(
    packed, cum, cum_t, scales, seg, level_states, skip, expand, *, state_dim, head_dim
):
    A, tok, width = packed.shape
    cg = expand.shape[1]
    hg = cum.shape[2]
    bits = len(level_states)

    def shard_spec(*dims):
        return pl.BlockSpec((1,) + dims, lambda s: (s, 0, 0))

    def sibling_spec(b):
        return pl.BlockSpec(
            (1, state_dim, cg), lambda s: (jnp.maximum(s // 2**b - 1, 0), 0, 0)
        )

    def whole_spec(shape):
        return pl.BlockSpec(shape, lambda s: (0, 0))

    return pl.pallas_call(
        lambda *refs: local_kernel(state_dim, head_dim, bits, *refs),
        grid=(A,),
        out_shape=jax.ShapeDtypeStruct((A * tok, cg), f32),
        in_specs=[
            shard_spec(tok, width),
            shard_spec(tok, hg),
            shard_spec(hg, tok),
            shard_spec(tok, scales.shape[2]),
            shard_spec(tok, 1),
            shard_spec(1, tok),
            whole_spec((1, cg)),
            whole_spec(expand.shape),
        ]
        + [sibling_spec(b) for b in range(bits)],
        out_specs=pl.BlockSpec((tok, cg), lambda s: (s, 0)),
        name="local_mix",
        cost_estimate=pl.CostEstimate(
            flops=1 << 32, bytes_accessed=12 << 20, transcendentals=1 << 21
        ),
    )(packed, cum, cum_t, scales, seg[:, :, None], seg[:, None, :], skip, expand, *level_states)


def gate_kernel(levels, packed_ref, mixed_ref, scale_ref, gates_ref, gain_ref, expand_ref, *rest):
    others, (hidden_ref, square_ref) = rest[:levels], rest[levels:]
    hg = expand_ref.shape[0]
    q = packed_ref[0]
    expand = expand_ref[...]
    scales = scale_ref[0]
    acc = mixed_ref[...]
    for level in range(levels):
        read = jnp.dot(q, others[level][...], preferred_element_type=f32)
        acc = acc + read * spread(scales[:, level * hg : (level + 1) * hg], expand)
    gate = gates_ref[0].astype(f32)
    gated = acc * (gate / (1.0 + jnp.exp(-gate)))
    square_ref[0] = jnp.sum(gated * gated, axis=1, keepdims=True)
    hidden_ref[...] = (gated * gain_ref[...]).astype(bf16)


def gate_call(packed, mixed, others, other_scales, gates, gain, expand, *, state_dim):
    A, tok, cg = gates.shape
    levels = len(others)
    scales = jnp.concatenate(other_scales, axis=2)

    def shard_spec(*dims):
        return pl.BlockSpec((1,) + dims, lambda s: (s, 0, 0))

    def whole_spec(shape):
        return pl.BlockSpec(shape, lambda s: (0, 0))

    rows_spec = pl.BlockSpec((tok, cg), lambda s: (s, 0))
    return pl.pallas_call(
        lambda *refs: gate_kernel(levels, *refs),
        grid=(A,),
        out_shape=[
            jax.ShapeDtypeStruct((A * tok, cg), bf16),
            jax.ShapeDtypeStruct((A, tok, 1), f32),
        ],
        in_specs=[
            shard_spec(tok, state_dim),
            rows_spec,
            shard_spec(tok, scales.shape[2]),
            shard_spec(tok, cg),
            whole_spec((1, cg)),
            whole_spec(expand.shape),
        ]
        + [whole_spec((state_dim, cg))] * levels,
        out_specs=[rows_spec, shard_spec(tok, 1)],
        name="gate_mix",
        cost_estimate=pl.CostEstimate(
            flops=1 << 30, bytes_accessed=8 << 20, transcendentals=1 << 20
        ),
    )(packed, mixed, scales, gates, gain, expand, *others)


def per_device(
    queries,
    key_rows,
    values,
    gate_rows,
    log_decay,
    skip_gain,
    lam_index,
    segments,
    lam_table,
    norm_gain,
    out_proj,
):
    tok, state_dim = queries.shape
    head_count = log_decay.shape[1]
    cols = values.shape[1]
    head_dim = cols // head_count
    classes, level_count = lam_table.shape[:2]
    dev_count = lax.axis_size("seq")
    inner_total = cols * lax.axis_size("head")
    A = math.gcd(math.gcd(head_count, 8), dev_count)
    Z = dev_count // A
    a_bits = A.bit_length() - 1
    z_bits = Z.bit_length() - 1
    hg = head_count // A
    cg = hg * head_dim
    rows = A * tok
    out_cols = out_proj.shape[1]
    groups = [[z * A + i for i in range(A)] for z in range(Z)]
    me = lax.axis_index("seq")
    in_pos = lax.rem(me, A)
    z_pos = lax.div(me, A)

    def exchange(blocks):
        return lax.all_to_all(
            blocks, "seq", 0, 0, tiled=True, axis_index_groups=groups
        )

    def my_heads(array, width, axis):
        return lax.dynamic_slice_in_dim(array, in_pos * width, width, axis)

    w_blocks = out_proj.T.reshape(out_cols, A, cg).swapaxes(0, 1)
    w_block = exchange(w_blocks).reshape(A * out_cols, cg)

    packed = pack_call(
        queries,
        key_rows,
        values,
        log_decay,
        lam_index.astype(f32)[:, None],
        segments.astype(f32)[:, None],
        groups=A,
    )
    packed = exchange(packed)

    def shift(block, step):
        pairs = [(p, (p + step * A) % dev_count) for p in range(dev_count)]
        return lax.ppermute(block, "seq", pairs)

    w_ring = [(0, w_block)]
    above = below = w_block
    if Z > 1:
        above = shift(w_block, 1)
        w_ring.append((1, above))
    if Z > 2:
        below = shift(w_block, -1)
        w_ring.append((-1, below))

    expand = (
        jnp.arange(hg, dtype=jnp.int32)[:, None]
        == jnp.arange(cg, dtype=jnp.int32)[None, :] // head_dim
    ).astype(bf16)
    *level_states, state = state_call(packed, expand, state_dim=state_dim, bits=a_bits)
    tail, state = lax.optimization_barrier((packed[:, :, 2 * state_dim + cg :], state))
    small = tail.astype(f32)
    cum = small[:, :, :hg] + small[:, :, hg : 2 * hg] + small[:, :, 2 * hg : 3 * hg]
    lam = small[:, :, 3 * hg].reshape(rows).astype(jnp.int32)
    seg = small[:, :, 3 * hg + 1]
    span = cum[:, -1, :]
    onehot = (lam[:, None] == jnp.arange(classes, dtype=jnp.int32)[None, :]).astype(f32)
    table = my_heads(lam_table, hg, 2).reshape(classes, level_count * hg)
    lw = jnp.dot(onehot, table, precision=highest).reshape(A, tok, level_count * hg)
    total = span
    prefix = jnp.zeros((A, hg), f32)
    prefixes = []
    for b in range(a_bits):
        wide = 2**b
        low_total, up_total = total[0::2], total[1::2]
        is_up = (jnp.arange(A, dtype=jnp.int32) // wide % 2 == 1)[:, None]
        prefixes.append(jnp.where(is_up, prefix, -jnp.inf))
        prefix = prefix + jnp.where(is_up, jnp.repeat(low_total, 2 * wide, axis=0), 0.0)
        total = low_total + up_total
    total = total[0]

    def level_scale(before, level):
        weight = lw[:, :, (2 + level) * hg : (3 + level) * hg]
        return jnp.exp(cum + before[:, None, :]) * weight

    gate_blocks = gate_rows.reshape(tok, A, cg).swapaxes(0, 1)
    gate_blocks, state, total = lax.optimization_barrier((gate_blocks, state, total))
    gates = exchange(gate_blocks)
    local_scales = [lw[:, :, : 2 * hg]]
    local_scales += [level_scale(before, b) for b, before in enumerate(prefixes)]
    local_scales = jnp.concatenate(local_scales, axis=2)

    others, other_scales = [], []
    local_packed = packed
    for zb in range(z_bits):
        other = xor_permute(state, A << zb)
        other_total = xor_permute(total[None, :], A << zb)[0]
        is_up = jnp.bitwise_and(jnp.right_shift(z_pos, zb), 1) == 1
        others.append(other)
        before = jnp.where(is_up, prefix, -jnp.inf)
        other_scales.append(level_scale(before, a_bits + zb))
        if zb + 1 < z_bits:
            up_state = jnp.where(is_up, state, other).astype(f32)
            low_state = jnp.where(is_up, other, state).astype(f32)
            factor = widen(jnp.exp(jnp.where(is_up, total, other_total)), head_dim)
            state = (up_state + factor[None, :] * low_state).astype(bf16)
            local_packed, state = lax.optimization_barrier((local_packed, state))
            prefix = prefix + jnp.where(is_up, other_total, 0.0)[None, :]
            total = total + other_total

    for distance in range(2, Z // 2 + 1):
        above, others = lax.optimization_barrier((above, others))
        above = shift(above, 1)
        w_ring.append((distance, above))
        if 2 * distance < Z:
            below = shift(below, -1)
            w_ring.append((-distance, below))

    skip = widen(my_heads(skip_gain, hg, 0), head_dim)[None, :]
    mixed = local_call(
        local_packed, cum, cum.swapaxes(1, 2), local_scales, seg, level_states, skip, expand,
        state_dim=state_dim, head_dim=head_dim,
    )
    gain = my_heads(norm_gain, cg, 0)[None, :]
    hidden, squares = gate_call(
        packed, mixed, others, other_scales, gates, gain, expand, state_dim=state_dim
    )

    def reduce_group(part, order, narrow):
        left = list(range(a_bits))[::-1]
        part = part.reshape((2,) * a_bits + part.shape[1:])
        for b in order:
            axis = left.index(b)
            left.remove(b)
            bit = jnp.bitwise_and(jnp.right_shift(in_pos, b), 1)
            mine = lax.dynamic_index_in_dim(part, bit, axis, keepdims=False)
            theirs = lax.dynamic_index_in_dim(part, 1 - bit, axis, keepdims=False)
            part = mine + xor_permute(theirs.astype(narrow), 2**b).astype(f32)
        return part

    bits = list(range(a_bits))
    flipped = bits[:1] + bits[1:][::-1]
    square_sum = reduce_group(squares.reshape(A, tok), bits, f32)
    square_sum = lax.psum(square_sum, "head")
    inv_rms = lax.rsqrt(square_sum / inner_total + epsilon)[:, None]
    block_cols = A * out_cols
    out = jnp.zeros((tok, Z * block_cols), bf16)
    for step, (distance, w_part) in enumerate(w_ring):
        part = lax.dot_general(
            hidden, w_part, (((1,), (1,)), ((), ())), preferred_element_type=f32
        )
        part = reduce_group(
            part.reshape(A, tok, block_cols), flipped if step % 2 else bits, bf16
        )
        block = lax.rem(z_pos - distance + Z, Z)
        out = lax.dynamic_update_slice_in_dim(
            out, (part * inv_rms).astype(bf16), block * block_cols, 1
        )
    return lax.psum_scatter(out, "head", scatter_dimension=0, tiled=True)


def solution(mesh):
    return jax.shard_map(
        per_device,
        mesh=mesh,
        in_specs=(
            P("seq", None),
            P("seq", None),
            P("seq", "head"),
            P("seq", "head"),
            P("seq", "head"),
            P("head"),
            P("seq"),
            P("seq"),
            P(None, None, "head"),
            P("head"),
            P("head", "seq"),
        ),
        out_specs=P(("seq", "head"), None),
        check_vma=False,
    )
```

```python
import math

import jax
import jax.numpy as jnp
from jax import lax
from jax.experimental import pallas as pl
from jax.experimental.pallas import tpu as pltpu
from jax.sharding import PartitionSpec as P

epsilon = 1e-05
highest = lax.Precision.HIGHEST
f32 = jnp.float32
bf16 = jnp.bfloat16


def xor_permute(value, mask):
    pairs = [(source, source ^ mask) for source in range(lax.axis_size("seq"))]
    return lax.ppermute(value, "seq", pairs)


def widen(matrix, head_dim):
    return jnp.repeat(matrix, head_dim, axis=-1)


def pack_kernel(groups, q_ref, k_ref, x_ref, decay_ref, lam_ref, seg_ref, out_ref):
    tok, state_dim = q_ref.shape
    cg = x_ref.shape[1] // groups
    hg = decay_ref.shape[1] // groups
    t_pos = lax.broadcasted_iota(jnp.int32, (tok, tok), 0)
    j_pos = lax.broadcasted_iota(jnp.int32, (tok, tok), 1)
    ones = jnp.where(t_pos >= j_pos, 1.0, 0.0).astype(f32)
    cum = jnp.dot(ones, decay_ref[...], precision=highest, preferred_element_type=f32)
    first = cum.astype(bf16).astype(f32)
    second = (cum - first).astype(bf16).astype(f32)
    third = cum - first - second
    pad = out_ref.shape[2] - 2 * state_dim - cg - 3 * hg - 2
    tail = [lam_ref[...], seg_ref[...], jnp.zeros((tok, pad), f32)]
    for s in range(groups):
        out_ref[s, :, :state_dim] = q_ref[...]
        out_ref[s, :, state_dim : 2 * state_dim] = k_ref[...]
        out_ref[s, :, 2 * state_dim : 2 * state_dim + cg] = x_ref[:, s * cg : (s + 1) * cg]
        parts = [part[:, s * hg : (s + 1) * hg] for part in (first, second, third)]
        small = jnp.concatenate(parts + tail, axis=1)
        out_ref[s, :, 2 * state_dim + cg :] = small.astype(bf16)


def pack_call(queries, key_rows, values, log_decay, lam, seg, *, groups):
    tok, state_dim = queries.shape
    width = 2 * state_dim + values.shape[1] // groups + 3 * (log_decay.shape[1] // groups) + 2
    vmem = pl.BlockSpec(memory_space=pltpu.VMEM)
    return pl.pallas_call(
        lambda *refs: pack_kernel(groups, *refs),
        out_shape=jax.ShapeDtypeStruct((groups, tok, pl.cdiv(width + 1, 128) * 128), bf16),
        in_specs=[vmem] * 6,
        out_specs=vmem,
        name="pack",
        cost_estimate=pl.CostEstimate(
            flops=1 << 22, bytes_accessed=4 << 20, transcendentals=0
        ),
    )(queries, key_rows, values, log_decay, lam, seg)


def spread(scale, expand):
    high = scale.astype(bf16)
    low = (scale - high.astype(f32)).astype(bf16)
    return jnp.dot(high, expand, preferred_element_type=f32) + jnp.dot(
        low, expand, preferred_element_type=f32
    )


def state_kernel(bits, state_dim, packed_ref, scale_ref, up_ref, expand_ref, *outs):
    A = packed_ref.shape[0]
    expand = expand_ref[...]
    up_wide = spread(up_ref[...], expand)
    for s in range(A):
        decayed = packed_ref[s, :, 2 * state_dim : 2 * state_dim + expand.shape[1]].astype(f32) * spread(scale_ref[s], expand)
        keys = packed_ref[s, :, state_dim : 2 * state_dim]
        outs[0][s] = lax.dot_general(
            keys,
            decayed.astype(bf16),
            (((0,), (0,)), ((), ())),
            preferred_element_type=f32,
        ).astype(bf16)
    row = 0
    for b in range(bits):
        for g in range(A >> (b + 1)):
            low = outs[b][2 * g].astype(f32)
            high = outs[b][2 * g + 1].astype(f32)
            merged = (high + up_wide[row : row + 1] * low).astype(bf16)
            if b + 1 < bits:
                outs[b + 1][g] = merged
            else:
                outs[b + 1][...] = merged
            row += 1


def state_call(packed, end_scale, up_rows, expand, *, state_dim, bits):
    A = packed.shape[0]
    cg = expand.shape[1]
    shapes = [(A >> b, state_dim, cg) for b in range(bits)] + [(state_dim, cg)]
    vmem = pl.BlockSpec(memory_space=pltpu.VMEM)
    return pl.pallas_call(
        lambda *refs: state_kernel(bits, state_dim, *refs),
        out_shape=[jax.ShapeDtypeStruct(shape, bf16) for shape in shapes],
        in_specs=[vmem] * 4,
        out_specs=[vmem] * len(shapes),
        name="group_states",
        cost_estimate=pl.CostEstimate(
            flops=1 << 29, bytes_accessed=8 << 20, transcendentals=0
        ),
    )(packed, end_scale, up_rows, expand)


def local_kernel(
    state_dim, head_dim, bits, packed_ref, cum_ref, cum_t_ref, scale_ref, seg_ref,
    seg_t_ref, skip_ref, expand_ref, *rest
):
    states, out_ref = rest[:bits], rest[bits]
    tok, hg = cum_ref.shape[1:]
    cg = expand_ref.shape[1]
    q = packed_ref[0, :, :state_dim]
    keys = packed_ref[0, :, state_dim : 2 * state_dim]
    expand = expand_ref[...]
    scores = lax.dot_general(
        q, keys, (((1,), (1,)), ((), ())), preferred_element_type=f32
    )
    same = seg_ref[0] == seg_t_ref[0]
    t_pos = lax.broadcasted_iota(jnp.int32, (tok, tok), 0)
    j_pos = lax.broadcasted_iota(jnp.int32, (tok, tok), 1)
    causal = t_pos >= j_pos
    scales = scale_ref[0]
    cum = cum_ref[0]
    cum_t = cum_t_ref[0]
    x_wide = packed_ref[0, :, 2 * state_dim : 2 * state_dim + cg]
    acc = skip_ref[...] * x_wide.astype(f32)
    for b in range(bits):
        read = jnp.dot(q, states[b][0], preferred_element_type=f32)
        acc = acc + read * spread(scales[:, (2 + b) * hg : (3 + b) * hg], expand)
    out_ref[...] = acc

    def head_weights(h):
        gaps = jnp.where(causal, cum[:, h : h + 1] - cum_t[h : h + 1, :], -jnp.inf)
        level_w = jnp.where(same, scales[:, h : h + 1], scales[:, hg + h : hg + h + 1])
        return (scores * jnp.exp(gaps) * level_w).astype(bf16)

    per_tile = max(1, 128 // head_dim)
    for first in range(0, hg, per_tile):
        heads = range(first, min(first + per_tile, hg))
        low, high = first * head_dim, min((first + per_tile) * head_dim, cg)
        x_tile = x_wide[:, low:high]
        lane_head = lax.broadcasted_iota(jnp.int32, (tok, high - low), 1) // head_dim
        tile = None
        for h in heads:
            part = jnp.dot(head_weights(h), x_tile, preferred_element_type=f32)
            tile = part if tile is None else jnp.where(lane_head == h - first, part, tile)
        out_ref[:, low:high] += tile


def local_call(
    packed, cum, cum_t, scales, seg, level_states, skip, expand, *, state_dim, head_dim
):
    A, tok, width = packed.shape
    cg = expand.shape[1]
    hg = cum.shape[2]
    bits = len(level_states)

    def shard_spec(*dims):
        return pl.BlockSpec((1,) + dims, lambda s: (s, 0, 0))

    def sibling_spec(b):
        return pl.BlockSpec(
            (1, state_dim, cg), lambda s: (jnp.maximum(s // 2**b - 1, 0), 0, 0)
        )

    def whole_spec(shape):
        return pl.BlockSpec(shape, lambda s: (0, 0))

    return pl.pallas_call(
        lambda *refs: local_kernel(state_dim, head_dim, bits, *refs),
        grid=(A,),
        out_shape=jax.ShapeDtypeStruct((A * tok, cg), f32),
        in_specs=[
            shard_spec(tok, width),
            shard_spec(tok, hg),
            shard_spec(hg, tok),
            shard_spec(tok, scales.shape[2]),
            shard_spec(tok, 1),
            shard_spec(1, tok),
            whole_spec((1, cg)),
            whole_spec(expand.shape),
        ]
        + [sibling_spec(b) for b in range(bits)],
        out_specs=pl.BlockSpec((tok, cg), lambda s: (s, 0)),
        name="local_mix",
        cost_estimate=pl.CostEstimate(
            flops=1 << 32, bytes_accessed=12 << 20, transcendentals=1 << 21
        ),
    )(packed, cum, cum_t, scales, seg[:, :, None], seg[:, None, :], skip, expand, *level_states)


def gate_kernel(levels, packed_ref, mixed_ref, scale_ref, gates_ref, gain_ref, expand_ref, *rest):
    others, (hidden_ref, square_ref) = rest[:levels], rest[levels:]
    hg = expand_ref.shape[0]
    q = packed_ref[0]
    expand = expand_ref[...]
    scales = scale_ref[0]
    acc = mixed_ref[...]
    for level in range(levels):
        read = jnp.dot(q, others[level][...], preferred_element_type=f32)
        acc = acc + read * spread(scales[:, level * hg : (level + 1) * hg], expand)
    gate = gates_ref[0].astype(f32)
    gated = acc * (gate / (1.0 + jnp.exp(-gate)))
    square_ref[0] = jnp.sum(gated * gated, axis=1, keepdims=True)
    hidden_ref[...] = (gated * gain_ref[...]).astype(bf16)


def gate_call(packed, mixed, others, other_scales, gates, gain, expand, *, state_dim):
    A, tok, cg = gates.shape
    levels = len(others)
    scales = jnp.concatenate(other_scales, axis=2)

    def shard_spec(*dims):
        return pl.BlockSpec((1,) + dims, lambda s: (s, 0, 0))

    def whole_spec(shape):
        return pl.BlockSpec(shape, lambda s: (0, 0))

    rows_spec = pl.BlockSpec((tok, cg), lambda s: (s, 0))
    return pl.pallas_call(
        lambda *refs: gate_kernel(levels, *refs),
        grid=(A,),
        out_shape=[
            jax.ShapeDtypeStruct((A * tok, cg), bf16),
            jax.ShapeDtypeStruct((A, tok, 1), f32),
        ],
        in_specs=[
            shard_spec(tok, state_dim),
            rows_spec,
            shard_spec(tok, scales.shape[2]),
            shard_spec(tok, cg),
            whole_spec((1, cg)),
            whole_spec(expand.shape),
        ]
        + [whole_spec((state_dim, cg))] * levels,
        out_specs=[rows_spec, shard_spec(tok, 1)],
        name="gate_mix",
        cost_estimate=pl.CostEstimate(
            flops=1 << 30, bytes_accessed=8 << 20, transcendentals=1 << 20
        ),
    )(packed, mixed, scales, gates, gain, expand, *others)


def per_device(
    queries,
    key_rows,
    values,
    gate_rows,
    log_decay,
    skip_gain,
    lam_index,
    segments,
    lam_table,
    norm_gain,
    out_proj,
):
    tok, state_dim = queries.shape
    head_count = log_decay.shape[1]
    cols = values.shape[1]
    head_dim = cols // head_count
    classes, level_count = lam_table.shape[:2]
    dev_count = lax.axis_size("seq")
    inner_total = cols * lax.axis_size("head")
    A = math.gcd(math.gcd(head_count, 8), dev_count)
    Z = dev_count // A
    a_bits = A.bit_length() - 1
    z_bits = Z.bit_length() - 1
    hg = head_count // A
    cg = hg * head_dim
    rows = A * tok
    out_cols = out_proj.shape[1]
    groups = [[z * A + i for i in range(A)] for z in range(Z)]
    me = lax.axis_index("seq")
    in_pos = lax.rem(me, A)
    z_pos = lax.div(me, A)

    def exchange(blocks):
        return lax.all_to_all(
            blocks, "seq", 0, 0, tiled=True, axis_index_groups=groups
        )

    def my_heads(array, width, axis):
        return lax.dynamic_slice_in_dim(array, in_pos * width, width, axis)

    w_blocks = out_proj.T.reshape(out_cols, A, cg).swapaxes(0, 1)
    w_block = exchange(w_blocks).reshape(A * out_cols, cg)

    packed = pack_call(
        queries,
        key_rows,
        values,
        log_decay,
        lam_index.astype(f32)[:, None],
        segments.astype(f32)[:, None],
        groups=A,
    )
    packed = exchange(packed)
    small = packed[:, :, 2 * state_dim + cg :].astype(f32)

    def shift(block, step):
        pairs = [(p, (p + step * A) % dev_count) for p in range(dev_count)]
        return lax.ppermute(block, "seq", pairs)

    w_ring = [(0, w_block)]
    above = below = w_block
    if Z > 1:
        above = shift(w_block, 1)
        w_ring.append((1, above))
    if Z > 2:
        below = shift(w_block, -1)
        w_ring.append((-1, below))

    cum = small[:, :, :hg] + small[:, :, hg : 2 * hg] + small[:, :, 2 * hg : 3 * hg]
    lam = small[:, :, 3 * hg].reshape(rows).astype(jnp.int32)
    seg = small[:, :, 3 * hg + 1]
    span = cum[:, -1, :]
    onehot = (lam[:, None] == jnp.arange(classes, dtype=jnp.int32)[None, :]).astype(f32)
    table = my_heads(lam_table, hg, 2).reshape(classes, level_count * hg)
    lw = jnp.dot(onehot, table, precision=highest).reshape(A, tok, level_count * hg)
    expand = (
        jnp.arange(hg, dtype=jnp.int32)[:, None]
        == jnp.arange(cg, dtype=jnp.int32)[None, :] // head_dim
    ).astype(bf16)

    total = span
    prefix = jnp.zeros((A, hg), f32)
    prefixes = []
    up_factors = []
    for b in range(a_bits):
        wide = 2**b
        low_total, up_total = total[0::2], total[1::2]
        is_up = (jnp.arange(A, dtype=jnp.int32) // wide % 2 == 1)[:, None]
        prefixes.append(jnp.where(is_up, prefix, -jnp.inf))
        up_factors.append(jnp.exp(up_total))
        prefix = prefix + jnp.where(is_up, jnp.repeat(low_total, 2 * wide, axis=0), 0.0)
        total = low_total + up_total
    total = total[0]

    def level_scale(before, level):
        weight = lw[:, :, (2 + level) * hg : (3 + level) * hg]
        return jnp.exp(cum + before[:, None, :]) * weight

    end_scale = jnp.exp(span[:, None, :] - cum)
    up_rows = jnp.concatenate(up_factors, axis=0)
    *level_states, state = state_call(
        packed, end_scale, up_rows, expand, state_dim=state_dim, bits=a_bits
    )
    gate_blocks = gate_rows.reshape(tok, A, cg).swapaxes(0, 1)
    gate_blocks, state, total = lax.optimization_barrier((gate_blocks, state, total))
    gates = exchange(gate_blocks)
    local_scales = [lw[:, :, : 2 * hg]]
    local_scales += [level_scale(before, b) for b, before in enumerate(prefixes)]
    local_scales = jnp.concatenate(local_scales, axis=2)

    others, other_scales = [], []
    local_packed = packed
    for zb in range(z_bits):
        other = xor_permute(state, A << zb)
        other_total = xor_permute(total[None, :], A << zb)[0]
        is_up = jnp.bitwise_and(jnp.right_shift(z_pos, zb), 1) == 1
        others.append(other)
        before = jnp.where(is_up, prefix, -jnp.inf)
        other_scales.append(level_scale(before, a_bits + zb))
        if zb + 1 < z_bits:
            up_state = jnp.where(is_up, state, other).astype(f32)
            low_state = jnp.where(is_up, other, state).astype(f32)
            factor = widen(jnp.exp(jnp.where(is_up, total, other_total)), head_dim)
            state = (up_state + factor[None, :] * low_state).astype(bf16)
            local_packed, state = lax.optimization_barrier((local_packed, state))
            prefix = prefix + jnp.where(is_up, other_total, 0.0)[None, :]
            total = total + other_total

    for distance in range(2, Z // 2 + 1):
        above, others = lax.optimization_barrier((above, others))
        above = shift(above, 1)
        w_ring.append((distance, above))
        if 2 * distance < Z:
            below = shift(below, -1)
            w_ring.append((-distance, below))

    skip = widen(my_heads(skip_gain, hg, 0), head_dim)[None, :]
    mixed = local_call(
        local_packed, cum, cum.swapaxes(1, 2), local_scales, seg, level_states, skip, expand,
        state_dim=state_dim, head_dim=head_dim,
    )
    gain = my_heads(norm_gain, cg, 0)[None, :]
    hidden, squares = gate_call(
        packed, mixed, others, other_scales, gates, gain, expand, state_dim=state_dim
    )

    def reduce_group(part, order, narrow):
        left = list(range(a_bits))[::-1]
        part = part.reshape((2,) * a_bits + part.shape[1:])
        for b in order:
            axis = left.index(b)
            left.remove(b)
            bit = jnp.bitwise_and(jnp.right_shift(in_pos, b), 1)
            mine = lax.dynamic_index_in_dim(part, bit, axis, keepdims=False)
            theirs = lax.dynamic_index_in_dim(part, 1 - bit, axis, keepdims=False)
            part = mine + xor_permute(theirs.astype(narrow), 2**b).astype(f32)
        return part

    bits = list(range(a_bits))
    flipped = bits[:1] + bits[1:][::-1]
    square_sum = reduce_group(squares.reshape(A, tok), bits, f32)
    square_sum = lax.psum(square_sum, "head")
    inv_rms = lax.rsqrt(square_sum / inner_total + epsilon)[:, None]
    block_cols = A * out_cols
    out = jnp.zeros((tok, Z * block_cols), bf16)
    for step, (distance, w_part) in enumerate(w_ring):
        part = lax.dot_general(
            hidden, w_part, (((1,), (1,)), ((), ())), preferred_element_type=f32
        )
        part = reduce_group(
            part.reshape(A, tok, block_cols), flipped if step % 2 else bits, bf16
        )
        block = lax.rem(z_pos - distance + Z, Z)
        out = lax.dynamic_update_slice_in_dim(
            out, (part * inv_rms).astype(bf16), block * block_cols, 1
        )
    return lax.psum_scatter(out, "head", scatter_dimension=0, tiled=True)


def solution(mesh):
    return jax.shard_map(
        per_device,
        mesh=mesh,
        in_specs=(
            P("seq", None),
            P("seq", None),
            P("seq", "head"),
            P("seq", "head"),
            P("seq", "head"),
            P("head"),
            P("seq"),
            P("seq"),
            P(None, None, "head"),
            P("head"),
            P("head", "seq"),
        ),
        out_specs=P(("seq", "head"), None),
        check_vma=False,
    )
```
